512 devices in a mesh: tok: 64 (over y, z), head: 8 (over x, core).
Axes of the slice: x: 4, y: 8, z: 8, core: 2. Of those that a mesh axis runs over, the one named last changes fastest.
Arguments:
- query_rows: bfloat16 [32768, 4096], P('tok', 'head'), may hold values from -8 to 8
- key_rows: bfloat16 [32768, 1024], P('tok', 'head'), may hold values from -8 to 8
- value_rows: bfloat16 [32768, 1024], P('tok', 'head'), may hold values from -12 to 12
- out_weight: bfloat16 [4096, 4096], P(None, 'head'), may hold values from -0.09375 to 0.09375
- doc_lengths: int32 [32], replicated, may hold values from 1 to 8192, 32768 in all
Outputs:
- mixed: bfloat16 [32768, 4096], P('tok', 'head')
The draws below stay inside these ranges and needn't reach their ends.
Inputs may be any that keep to these rules, and one draw needn't show every extreme that they name: `doc_lengths`: the lengths sum to 32768 and the longest document has exactly 8192 tokens.
All inputs are finite; a program needn't handle non-finite values.
Results may differ from the reference program's by a relative error of at most 0.0053.
Values may be sent and summed in bfloat16 or wider, within the bound.
No kernel may reach another device: no remote copies, remote signals or barrier semaphores. Data moves between devices by JAX's collectives and lax.ppermute only.
A program may use at most 64 MiB of HBM per device.

```python
import math
import jax
import jax.numpy as jnp
import numpy as np
from jax import lax

D = 4096
QHEADS = 32
KVH = 8
HD = 128
TILE = 128
TOKENS = 32768
MAXDOC = 8192
NDOCS = 32


def draw_query_rows(key, part):
    own_key = jax.random.fold_in(key, 11)
    result = jnp.clip(jax.random.normal(own_key, (TOKENS, QHEADS * HD)), -6.0, 6.0)
    return result.astype(jnp.bfloat16)


def draw_key_rows(key, part):
    own_key = jax.random.fold_in(key, 23)
    result = jnp.clip(jax.random.normal(own_key, (TOKENS, KVH * HD)), -6.0, 6.0)
    return result.astype(jnp.bfloat16)


def levels(key, shape, cuts, low, largest):
    def one(dim, blocks):
        steps = jax.random.uniform(jax.random.fold_in(jax.random.fold_in(key, 6), dim), (blocks,), jnp.float32, low / len(cuts), largest / len(cuts))
        return jnp.repeat(jnp.exp(steps), shape[dim] // blocks).reshape((-1,) + (1,) * (len(shape) - dim - 1))

    factor_of = one(*cuts[0])
    for cut in cuts[1:]:
        factor_of = factor_of * one(*cut)
    return factor_of


def length_profile(number_of, total, reach, lean):
    portions = [(1 << 20) // math.isqrt(rank ** lean) + 1 for rank in range(2, number_of + 1)]
    spare, holding = total - reach - (number_of - 1), [1] * (number_of - 1)
    while spare > 0:
        candidates = [i for i in range(number_of - 1) if holding[i] < reach]
        pool, left = sum([portions[i] for i in candidates]), spare
        for i in candidates:
            more = min(reach - holding[i], max(1, left * portions[i] // pool), spare)
            holding[i] = holding[i] + more
            spare = spare - more
    return np.array([reach] + holding)


def uneven(key, amount, total, most, slope):
    if amount == 2:
        one = jax.random.randint(key, (), max(1, total - most), min(most, total - 1) + 1)
        return jnp.stack([one, total - one])
    sizes = jnp.asarray(length_profile(amount, total, most, slope), jnp.int32)
    pairs = (amount - 1) // 2
    giver, sink = sizes[1:1 + 2 * pairs:2], sizes[2:2 + 2 * pairs:2]
    slack = jnp.minimum(giver - 1, most - sink)
    shifted = jax.random.randint(jax.random.fold_in(key, 1), (pairs,), 0, 1 << 20) % (slack + 1)
    sizes = sizes.at[1:1 + 2 * pairs:2].set(giver - shifted).at[2:2 + 2 * pairs:2].set(sink + shifted)
    return sizes[jax.random.permutation(jax.random.fold_in(key, 2), amount)]


def gaussian(key, extent, spread, most, cuts=(), kind=jnp.bfloat16):
    array = spread * jax.random.normal(key, extent, jnp.float32)
    if cuts:
        array = array * levels(key, extent, cuts, -0.22, 0.18)
    return jnp.clip(array, -most, most).astype(kind)


def setup_inputs(seed: int = 0) -> dict:
    streams_of = jax.random.split(jax.random.key(seed), 6)
    return {
        "query_rows": draw_query_rows(jax.random.fold_in(streams_of[5], 71), 0),
        "key_rows": draw_key_rows(jax.random.fold_in(streams_of[5], 71), 0),
        "value_rows": gaussian(streams_of[2], (TOKENS, KVH * HD), 2.0, 12.0, ((0, 64), (1, 8))),
        "out_weight": gaussian(streams_of[3], (QHEADS * HD, D), (QHEADS * HD) ** -0.5, 0.09375, ((1, 8),)),
        "doc_lengths": uneven(streams_of[4], NDOCS, TOKENS, MAXDOC, 2).astype(jnp.int32),
    }


very_negative = -1e+30

def document_start(positions, doc_lengths):
    doc_ends = jnp.cumsum(doc_lengths).astype(jnp.int32)
    doc_starts = (doc_ends - doc_lengths).astype(jnp.int32)
    inside = (positions[:, None] >= doc_starts[None, :]) & (positions[:, None] < doc_ends[None, :])
    return lax.optimization_barrier(jnp.sum(jnp.where(inside, doc_starts[None, :], 0), axis=1)).astype(jnp.int32)

def reference(query_rows, key_rows, value_rows, out_weight, doc_lengths):
    group_size = QHEADS // KVH
    score_scale = 1.0 / math.sqrt(HD)
    tile_total = TOKENS // TILE
    window_len = MAXDOC + TILE
    padded_keys = jnp.concatenate([jnp.zeros((MAXDOC, KVH * HD), key_rows.dtype), key_rows], axis=0)
    padded_values = jnp.concatenate([jnp.zeros((MAXDOC, KVH * HD), value_rows.dtype), value_rows], axis=0)

    def tile_attention(tile_index):
        tile_first = (tile_index * TILE).astype(jnp.int32)
        queries = lax.dynamic_slice_in_dim(query_rows, tile_first, TILE, 0).astype(jnp.float32)
        queries = queries.reshape(TILE, KVH, group_size, HD)
        key_win = lax.dynamic_slice_in_dim(padded_keys, tile_first, window_len, 0).astype(jnp.float32)
        key_win = key_win.reshape(window_len, KVH, HD)
        value_win = lax.dynamic_slice_in_dim(padded_values, tile_first, window_len, 0).astype(jnp.float32)
        value_win = value_win.reshape(window_len, KVH, HD)
        row_pos = tile_first + jnp.arange(TILE, dtype=jnp.int32)
        doc_start = document_start(row_pos, doc_lengths)
        key_pos = tile_first - MAXDOC + jnp.arange(window_len, dtype=jnp.int32)
        allowed = (key_pos[None, :] >= doc_start[:, None]) & (key_pos[None, :] <= row_pos[:, None])
        scores = jnp.einsum('tcgd,kcd->cgtk', queries, key_win) * score_scale
        scores = jnp.where(allowed[None, None], scores, very_negative)
        running_max = lax.optimization_barrier(jnp.max(scores, axis=3))
        exponent = jnp.where(allowed[None, None], jnp.exp(scores - running_max[..., None]), 0.0)
        denominator = lax.optimization_barrier(jnp.sum(exponent, axis=3))
        weights = lax.optimization_barrier(exponent.astype(jnp.bfloat16))
        numerator = jnp.einsum('cgtk,kcd->tcgd', weights.astype(jnp.float32), value_win)
        output = numerator / jnp.transpose(denominator, (2, 0, 1))[..., None]
        return output.reshape(TILE, QHEADS * HD).astype(jnp.bfloat16)
    attended = lax.map(tile_attention, jnp.arange(tile_total, dtype=jnp.int32))
    attended = attended.reshape(TOKENS, QHEADS * HD)
    return jnp.dot(attended, out_weight, preferred_element_type=jnp.float32).astype(jnp.bfloat16)
```

```python
import functools
import math

import jax
import jax.numpy as jnp
from jax import lax
from jax.experimental import pallas as pl
from jax.experimental.pallas import tpu as pltpu
from jax.sharding import PartitionSpec as P

HD = 128
GROUP = 4
PIECE = 512
ROW = 8
NEG = -1e30
EXP_SCALE = math.log2(math.e) / math.sqrt(HD)


def query_bounds(place_ref, lens_ref, count):
    first = place_ref[0] * PIECE
    pos = first + lax.broadcasted_iota(jnp.int32, (1, PIECE), 1)

    def step(j, carried):
        at, start, start_first = carried
        start = jnp.where(pos >= at, at, start)
        start_first = jnp.where(first >= at, at, start_first)
        return (at + lens_ref[j], start, start_first)

    zero = jnp.int32(0)
    _, start, start_first = lax.fori_loop(0, count, step, (zero, jnp.zeros_like(pos), zero))
    return first, pos, start, start_first


def attend(q_ref, keys, values, m_ref, l_ref, acc_ref, allowed):
    for h in range(GROUP):
        cols = slice(h * HD, (h + 1) * HD)
        lanes = slice(h * PIECE, (h + 1) * PIECE)
        s = lax.dot_general(
            keys, q_ref[:, cols], (((1,), (1,)), ((), ())), preferred_element_type=jnp.float32
        )
        if allowed is not None:
            s = jnp.where(allowed, s, NEG)
        m_old = m_ref[:, lanes]
        m_new = jnp.maximum(m_old, jnp.max(s, axis=0, keepdims=True))
        p = jnp.exp2((s - m_new) * EXP_SCALE)
        alpha = jnp.exp2((m_old - m_new) * EXP_SCALE)
        m_ref[:, lanes] = m_new
        l_ref[:, lanes] = l_ref[:, lanes] * alpha + jnp.sum(p, axis=0, keepdims=True)
        o = lax.dot_general(
            values, p.astype(jnp.bfloat16), (((0,), (0,)), ((), ())), preferred_element_type=jnp.float32
        )
        acc_ref[:, lanes] = acc_ref[:, lanes] * alpha + o


def diagonal_kernel(place_ref, lens_ref, q_ref, kv_ref, m_ref, l_ref, acc_ref):
    first, pos, start, _ = query_bounds(place_ref, lens_ref, lens_ref.shape[0])
    m_ref[...] = jnp.full_like(m_ref, NEG)
    l_ref[...] = jnp.zeros_like(l_ref)
    acc_ref[...] = jnp.zeros_like(acc_ref)
    key_pos = first + lax.broadcasted_iota(jnp.int32, (PIECE, 1), 0)
    allowed = (key_pos >= start) & (key_pos <= pos)
    attend(q_ref, kv_ref[:, :HD], kv_ref[:, HD:], m_ref, l_ref, acc_ref, allowed)


def row_kernel(back, last, place_ref, lens_ref, q_ref, kv_ref, m_in, l_in, acc_in, *refs):
    if last:
        out_ref, m_ref, l_ref, acc_ref = refs
    else:
        m_ref, l_ref, acc_ref = refs
    first, pos, start, start_first = query_bounds(place_ref, lens_ref, lens_ref.shape[0])
    m_ref[...] = m_in[...]
    l_ref[...] = l_in[...]
    acc_ref[...] = acc_in[...]
    me = lax.rem(place_ref[0], ROW)
    needed = (first - start_first + PIECE - 1) // PIECE
    low = jnp.maximum(1, me + 1 + (back - 1) * ROW)
    high = jnp.minimum(needed, me + back * ROW)

    def step(distance, _):
        piece = me - distance + back * ROW
        rows = pl.ds(pl.multiple_of(piece * PIECE, PIECE), PIECE)
        keys = kv_ref[rows, :HD]
        values = kv_ref[rows, HD:]
        key_first = first - distance * PIECE
        whole = (key_first >= start_first) & (start_first + 0 >= start_last)

        @pl.when(whole)
        def _():
            attend(q_ref, keys, values, m_ref, l_ref, acc_ref, None)

        @pl.when(jnp.logical_not(whole))
        def _():
            key_pos = key_first + lax.broadcasted_iota(jnp.int32, (PIECE, 1), 0)
            attend(q_ref, keys, values, m_ref, l_ref, acc_ref, key_pos >= start)

        return 0

    start_last = jnp.max(start)
    lax.fori_loop(low, high + 1, step, 0)
    if last:
        for h in range(GROUP):
            lanes = slice(h * PIECE, (h + 1) * PIECE)
            o = acc_ref[:, lanes] / l_ref[:, lanes]
            out_ref[:, h * HD : (h + 1) * HD] = o.T.astype(jnp.bfloat16)


def state_shapes():
    lanes = GROUP * PIECE
    return [
        jax.ShapeDtypeStruct((1, lanes), jnp.float32),
        jax.ShapeDtypeStruct((1, lanes), jnp.float32),
        jax.ShapeDtypeStruct((HD, lanes), jnp.float32),
    ]


SMEM = pl.BlockSpec(memory_space=pltpu.SMEM)
VMEM = pl.BlockSpec(memory_space=pltpu.VMEM)


def attention_cost(pieces):
    flops = 4 * pieces * PIECE * GROUP * PIECE * HD
    return pl.CostEstimate(flops=flops, bytes_accessed=4 << 20, transcendentals=pieces * GROUP * PIECE * PIECE)


def diagonal(place, lens, q, kv):
    return pl.pallas_call(
        diagonal_kernel,
        out_shape=state_shapes(),
        in_specs=[SMEM, SMEM, VMEM, VMEM],
        out_specs=[VMEM] * 3,
        cost_estimate=attention_cost(1),
        name="diagonal",
    )(place, lens, q, kv)


def row(back, last, place, lens, q, kv, state):
    lanes = GROUP * PIECE
    if last:
        out_shape = jax.ShapeDtypeStruct((PIECE, GROUP * HD), jnp.bfloat16)
        out_specs = VMEM
        scratch = [
            pltpu.VMEM((1, lanes), jnp.float32),
            pltpu.VMEM((1, lanes), jnp.float32),
            pltpu.VMEM((HD, lanes), jnp.float32),
        ]
    else:
        out_shape = state_shapes()
        out_specs = [VMEM] * 3
        scratch = []
    return pl.pallas_call(
        functools.partial(row_kernel, back, last),
        out_shape=out_shape,
        in_specs=[SMEM, SMEM] + [VMEM] * 5,
        out_specs=out_specs,
        scratch_shapes=scratch,
        cost_estimate=attention_cost(ROW),
        name="row%d" % back,
    )(place, lens, q, kv, *state)


def local(query_rows, key_rows, value_rows, out_weight, doc_lengths):
    count = lax.axis_size("tok")
    place = lax.axis_index("tok").astype(jnp.int32).reshape(1)
    rows = [list(range(r, r + ROW)) for r in range(0, count, ROW)]
    kv = jnp.concatenate([key_rows, value_rows], axis=1)
    behind1 = lax.ppermute(kv, "tok", [(i, i + ROW) for i in range(count - ROW)])
    behind2 = lax.ppermute(kv, "tok", [(i, i + 2 * ROW) for i in range(count - 2 * ROW)])

    def gather(x):
        return lax.all_gather(x, "tok", axis=0, tiled=True, axis_index_groups=rows)

    state = diagonal(place, doc_lengths, query_rows, kv)
    state = row(0, False, place, doc_lengths, query_rows, gather(kv), state)
    state = row(1, False, place, doc_lengths, query_rows, gather(behind1), state)
    attended = row(2, True, place, doc_lengths, query_rows, gather(behind2), state)
    mixed = jnp.dot(
        lax.all_gather(attended, "head", axis=1, tiled=True),
        out_weight,
        preferred_element_type=jnp.float32,
    )
    return mixed.astype(jnp.bfloat16)


def solution(mesh):
    return jax.shard_map(
        local,
        mesh=mesh,
        in_specs=(P("tok", "head"), P("tok", "head"), P("tok", "head"), P(None, "head"), P()),
        out_specs=P("tok", "head"),
        check_vma=False,
    )
```

```python
import functools
import math

import jax
import jax.numpy as jnp
from jax import lax
from jax.experimental import pallas as pl
from jax.experimental.pallas import tpu as pltpu
from jax.sharding import PartitionSpec as P

HD = 128
GROUP = 4
PIECE = 512
ROW = 8
NEG = -1e30
EXP_SCALE = math.log2(math.e) / math.sqrt(HD)
LANES = ((1,), (1,)), ((), ())
PLAIN = ((1,), (0,)), ((), ())


def query_bounds(place_ref, lens_ref):
    first = place_ref[0] * PIECE
    pos = first + lax.broadcasted_iota(jnp.int32, (1, PIECE), 1)

    def step(j, carried):
        at, start, start_first, start_last = carried
        start = jnp.where(pos >= at, at, start)
        start_first = jnp.where(first >= at, at, start_first)
        start_last = jnp.where(first + PIECE - 1 >= at, at, start_last)
        return (at + lens_ref[j], start, start_first, start_last)

    zero = jnp.int32(0)
    carried = (zero, jnp.zeros_like(pos), zero, zero)
    _, start, start_first, start_last = lax.fori_loop(0, lens_ref.shape[0], step, carried)
    return first, pos, start, start_first, start_last


def scores(q, keys):
    return lax.dot_general(keys, q, LANES, preferred_element_type=jnp.float32)


def absorb(s, values_t, head, state):
    m_ref, l_ref, acc_ref = state
    m_old = m_ref[head]
    m_new = jnp.maximum(m_old, jnp.max(s, axis=0, keepdims=True))
    p = jnp.exp2((s - m_new) * EXP_SCALE)
    alpha = jnp.exp2((m_old - m_new) * EXP_SCALE)
    m_ref[head] = m_new
    l_ref[head] = l_ref[head] * alpha + jnp.sum(p, axis=0, keepdims=True)
    o = lax.dot_general(values_t, p.astype(jnp.bfloat16), PLAIN, preferred_element_type=jnp.float32)
    acc_ref[head] = acc_ref[head] * alpha + o


def values_of(kv):
    return jnp.concatenate([kv[b * HD : (b + 1) * HD, HD:] for b in range(PIECE // HD)], axis=1)


def pack_kernel(k_ref, v_ref, kv_ref):
    kv_ref[0, :, :HD] = k_ref[...]
    for b in range(PIECE // HD):
        rows = slice(b * HD, (b + 1) * HD)
        kv_ref[0, rows, HD:] = v_ref[rows, :].T


def diagonal_kernel(place_ref, lens_ref, q_ref, kv_ref, m_ref, l_ref, acc_ref, qt_ref):
    first, pos, start, _, _ = query_bounds(place_ref, lens_ref)
    m_ref[...] = jnp.full_like(m_ref, NEG)
    l_ref[...] = jnp.zeros_like(l_ref)
    acc_ref[...] = jnp.zeros_like(acc_ref)
    key_pos = first + lax.broadcasted_iota(jnp.int32, (PIECE, 1), 0)
    allowed = (key_pos >= start) & (key_pos <= pos)
    kv = kv_ref[0]
    for h in range(GROUP):
        qt_ref[h] = q_ref[:, h * HD : (h + 1) * HD]
        s = jnp.where(allowed, scores(qt_ref[h], kv[:, :HD]), NEG)
        absorb(s, values_of(kv), h, (m_ref, l_ref, acc_ref))


def pieces_kernel(distance, slots, place_ref, lens_ref, q_ref, kv_ref, m_in, l_in, acc_in, m_ref, l_ref, acc_ref, s_even, s_odd):
    del m_in, l_in, acc_in
    first, _, start, start_first, start_last = query_bounds(place_ref, lens_ref)
    state = (m_ref, l_ref, acc_ref)
    buffers = (s_even, s_odd)

    def piece(slot, _):
        key_first = first - (distance + slot * ROW) * PIECE
        needed = key_first + PIECE > start_first
        whole = key_first >= start_last

        @pl.when(needed & whole)
        def _():
            s_even[...] = scores(q_ref[0], kv_ref[slot, :, :HD])
            for h in range(GROUP):
                if h + 1 < GROUP:
                    buffers[(h + 1) % 2][...] = scores(q_ref[h + 1], kv_ref[slot, :, :HD])
                absorb(buffers[h % 2][...], values_of(kv_ref[slot]), h, state)

        @pl.when(needed & jnp.logical_not(whole))
        def _():
            key_pos = key_first + lax.broadcasted_iota(jnp.int32, (PIECE, 1), 0)

            def one(h, _):
                s = jnp.where(key_pos >= start, scores(q_ref[h], kv_ref[slot, :, :HD]), NEG)
                absorb(s, values_of(kv_ref[slot]), h, state)
                return 0

            lax.fori_loop(0, GROUP, one, 0)

        return 0

    lax.fori_loop(0, slots, piece, 0)


def finish_kernel(l_ref, acc_ref, out_ref):
    for h in range(GROUP):
        o = acc_ref[h] / l_ref[h]
        out_ref[:, h * HD : (h + 1) * HD] = o.T.astype(jnp.bfloat16)


STATE = [
    jax.ShapeDtypeStruct((GROUP, 1, PIECE), jnp.float32),
    jax.ShapeDtypeStruct((GROUP, 1, PIECE), jnp.float32),
    jax.ShapeDtypeStruct((GROUP, HD, PIECE), jnp.float32),
]
SMEM = pl.BlockSpec(memory_space=pltpu.SMEM)
VMEM = pl.BlockSpec(memory_space=pltpu.VMEM)


def cost(pieces):
    flops = 4 * pieces * PIECE * GROUP * PIECE * HD
    return pl.CostEstimate(flops=flops, bytes_accessed=1 << 20, transcendentals=pieces * GROUP * PIECE * PIECE)


def params(mib):
    return pltpu.CompilerParams(vmem_limit_bytes=mib << 20)


def pack(k, v):
    return pl.pallas_call(
        pack_kernel,
        out_shape=jax.ShapeDtypeStruct((1, PIECE, 2 * HD), jnp.bfloat16),
        in_specs=[VMEM, VMEM],
        out_specs=VMEM,
        compiler_params=params(8),
        name="pack",
    )(k, v)


def diagonal(place, lens, q, kv):
    *state, qt = pl.pallas_call(
        diagonal_kernel,
        out_shape=STATE + [jax.ShapeDtypeStruct((GROUP, PIECE, HD), jnp.bfloat16)],
        in_specs=[SMEM, SMEM, VMEM, VMEM],
        out_specs=[VMEM] * 4,
        cost_estimate=cost(1),
        compiler_params=params(24),
        name="diagonal",
    )(place, lens, q, kv)
    return state, qt


def pieces(distance, place, lens, q, kv, state):
    slots = kv.shape[0]
    return pl.pallas_call(
        functools.partial(pieces_kernel, distance, slots),
        out_shape=STATE,
        in_specs=[SMEM, SMEM] + [VMEM] * 5,
        out_specs=[VMEM] * 3,
        scratch_shapes=[pltpu.VMEM((PIECE, PIECE), jnp.float32)] * 2,
        input_output_aliases={4: 0, 5: 1, 6: 2},
        cost_estimate=cost(slots),
        compiler_params=params(24),
        name="pieces%d" % distance,
    )(place, lens, q, kv, *state)


def finish(state):
    return pl.pallas_call(
        finish_kernel,
        out_shape=jax.ShapeDtypeStruct((PIECE, GROUP * HD), jnp.bfloat16),
        in_specs=[VMEM, VMEM],
        out_specs=VMEM,
        compiler_params=params(8),
        name="finish",
    )(state[1], state[2])


def shift(value, steps):
    count = lax.axis_size("tok")
    return lax.ppermute(value, "tok", [(i, (i + steps) % count) for i in range(count)])


def local(query_rows, key_rows, value_rows, out_weight, doc_lengths):
    place = lax.axis_index("tok").astype(jnp.int32).reshape(1)
    kv = pack(key_rows, value_rows)
    back8 = shift(kv, ROW)
    up = [shift(jnp.concatenate([kv, back8]), 1)]
    back16 = shift(back8, ROW)
    down = [shift(jnp.concatenate([back8, back16]), -1)]
    up.append(shift(up[-1], 1))
    down.append(shift(down[-1], -1))
    up.append(shift(up[-1], 1))
    down.append(shift(down[-1], -1))
    up.append(shift(up[-1], 1))

    state, q = diagonal(place, doc_lengths, query_rows, kv)
    order = [(8, back8), (16, back16), (1, up[0]), (7, down[0]), (2, up[1])]
    order += [(6, down[1]), (3, up[2]), (5, down[2]), (4, up[3])]
    for distance, arrived in order:
        state = pieces(distance, place, doc_lengths, q, arrived, state)
    mixed = jnp.dot(
        lax.all_gather(finish(state), "head", axis=1, tiled=True),
        out_weight,
        preferred_element_type=jnp.float32,
    )
    return mixed.astype(jnp.bfloat16)


def solution(mesh):
    return jax.shard_map(
        local,
        mesh=mesh,
        in_specs=(P("tok", "head"), P("tok", "head"), P("tok", "head"), P(None, "head"), P()),
        out_specs=P("tok", "head"),
        check_vma=False,
    )
```
